256 devices in a mesh: row: 32 (over z_lo, y, core), col: 8 (over z_hi, x).
Axes of the slice: x: 4, y: 4, z: 8 (z_hi: 2, z_lo: 4; z = z_hi * 4 + z_lo), core: 2. Of those that a mesh axis runs over, the one named last changes fastest.
Arguments:
- grads: bfloat16 [163840, 1024], P(('row', 'col')), may hold values from -120 to 120
- round_masks: int32 [2], replicated, may hold values from 1 to 30, as said below
Outputs:
- influence: float32 [2, 163840, 640], P(None, ('row', 'col'))
The draws below stay inside these ranges and needn't reach their ends.
Inputs may be any that keep to these rules, and one draw needn't show every extreme that they name: round_masks[1] equals round_masks[0] with all binary digits below 32 flipped, so the two rounds pair every block with two different partners.
All inputs are finite; a program needn't handle non-finite values.
Results may differ from the reference program's by a relative error of at most 0.0031.
The reference program's roundings to bfloat16 on the way (of `white`) count: a program that leaves them out, or rounds other values in their place, can miss the bound.
Values may be sent and summed in bfloat16 or wider, within the bound.
A program may use at most 128 MiB of HBM per device.

```python
import jax
import jax.numpy as jnp
from jax import lax

P_SIZE = 1024
EX = 640
ROUNDS = 2
ROW_SIDE = 32
NEX = 163840
N_ROW = 32
N_COL = 8


def draw_round_masks(key, part):
    coin = jax.random.randint(key, (1,), 0, 2).astype(jnp.int32)
    first_mask = (1 + coin * (ROW_SIDE - 3)).astype(jnp.int32)
    second_mask = jnp.bitwise_xor(first_mask, ROW_SIDE - 1).astype(jnp.int32)
    return jnp.concatenate([first_mask, second_mask], axis=0)


def draw_grads(key, part):
    key_noise = jax.random.fold_in(key, 11)
    key_column = jax.random.fold_in(key, 12)
    key_jitter = jax.random.fold_in(key, 13)
    block_total = NEX // EX
    column_scale = jnp.exp(jax.random.uniform(key_column, (1, P_SIZE), jnp.float32, -3.5, 2.5))
    block_place = (jnp.arange(NEX, dtype=jnp.int32) // EX).astype(jnp.float32)
    rising = jnp.sqrt(1.0 + 2.0 * block_place / max(block_total - 1, 1))[:, None]
    jitter = jnp.exp(jax.random.uniform(key_jitter, (block_total, P_SIZE), jnp.float32, -0.3, 0.3))
    jitter_rows = jnp.repeat(jitter, EX, axis=0)
    base = jnp.clip(jax.random.normal(key_noise, (NEX, P_SIZE), jnp.float32), -4.0, 4.0)
    return (base * column_scale * rising * jitter_rows).astype(jnp.bfloat16)


def setup_inputs(seed: int = 0) -> dict:
    keys = jax.random.split(jax.random.key(seed), 3)
    grads = draw_grads(jax.random.fold_in(keys[2], 71), 0)
    round_masks = draw_round_masks(jax.random.fold_in(keys[2], 71), 0)
    return {"grads": grads, "round_masks": round_masks}


DAMPING = 0.1

def whiten(rows, factor):
    solved = lax.linalg.triangular_solve(factor, rows.astype(jnp.float32), left_side=False, lower=True, transpose_a=True)
    return solved.astype(jnp.bfloat16)

def reference(grads, round_masks):
    gram = jnp.dot(grads.T.astype(jnp.float32), grads.astype(jnp.float32), preferred_element_type=jnp.float32)
    hessian = gram / NEX + DAMPING * jnp.eye(P_SIZE, dtype=jnp.float32)
    factor = jnp.linalg.cholesky(hessian)
    white = whiten(grads, factor)
    blocks = white.reshape(N_ROW, N_COL, EX, P_SIZE)
    scale = 1.0 / jnp.sqrt(jnp.float32(P_SIZE))
    indices = jnp.arange(N_ROW, dtype=jnp.int32)
    results = []
    for which_round in range(ROUNDS):
        round_mask = round_masks[which_round]

        def one_side(side_index):
            partner = jnp.bitwise_xor(side_index, round_mask).astype(jnp.int32)
            own_rows = lax.dynamic_index_in_dim(blocks, side_index, 0, keepdims=False)
            partner_rows = lax.dynamic_index_in_dim(blocks, partner, 0, keepdims=False)
            scores = jnp.einsum('cip,cjp->cij', own_rows.astype(jnp.float32), partner_rows.astype(jnp.float32))
            return scores * scale
        scored = lax.map(one_side, indices)
        results.append(scored.reshape(NEX, EX))
    return jnp.stack(results, axis=0)
```

```python
import functools

import jax
import jax.numpy as jnp
from jax import lax
from jax.experimental import pallas as pl
from jax.experimental.pallas import tpu as pltpu
from jax.sharding import PartitionSpec as P

DAMPING = 0.1

F32, BF = jnp.float32, jnp.bfloat16
NB = 128

def recip(x):
    return 1.0 / x

def factor_block(rows):
    lane = lax.broadcasted_iota(jnp.int32, (8, 128), 1)
    sub = lax.broadcasted_iota(jnp.int32, (8, 128), 0)
    M = list(rows)
    drow = jnp.ones((8, 128), F32)
    G = len(M)
    for g in range(G):
        base = 8 * g
        R = M[g]
        r = [jnp.broadcast_to(R[a:a+1, :], (8, 128)) for a in range(8)]
        s = {(a, b): jnp.broadcast_to(r[a][:, base+b:base+b+1], (8, 128)) for a in range(8) for b in range(a, 8)}
        l = {}
        f = [None] * 8
        for a in range(8):
            i = recip(s[a, a])
            drow = jnp.where(lane == base + a, s[a, a], drow)
            for b in range(a + 1, 8):
                l[a, b] = s[a, b] * i
                r[b] = r[b] - l[a, b] * r[a]
                for c in range(b, 8):
                    s[b, c] = s[b, c] - l[a, b] * s[a, c]
            f[a] = jnp.where(lane > base + a, r[a] * i, 0.0)
        h = list(f)
        for a in range(6, -1, -1):
            for b in range(a + 1, 8):
                h[a] = h[a] - l[a, b] * h[b]
        order = list(range(g + 1, G)) + list(range(g))
        for v in order:
            c = [jnp.broadcast_to(M[v][:, base+a:base+a+1], (8, 128)) for a in range(8)]
            t = c[0] * h[0]
            for a in range(1, 8):
                t = t + c[a] * h[a]
            M[v] = M[v] - t
        acc = jnp.where(lane == base + sub, 1.0, 0.0)
        hh = h[0]
        for a in range(1, 8):
            hh = jnp.where(sub == a, h[a], hh)
        M[g] = acc - hh
    y = lax.rsqrt(drow)
    y = y * (1.5 - 0.5 * drow * y * y)
    return [m * y for m in M]

def split2(x):
    hi = x.astype(BF)
    lo = (x - hi.astype(F32)).astype(BF)
    return hi, lo

def nt(a, b):
    return lax.dot_general(a, b, (((1,), (1,)), ((), ())), preferred_element_type=F32)

def nn(a, b):
    return lax.dot_general(a, b, (((1,), (0,)), ((), ())), preferred_element_type=F32)

def chol_kernel(inv_n, damping, h_ref, hi_ref, lo_ref, m_ref, xt_ref, p3_ref, q3_ref):
    n = m_ref.shape[0]
    K = n // NB
    @pl.loop(0, K)
    def _(k):
        kb = pl.multiple_of(k * NB, NB)
        eye = jnp.where(lax.broadcasted_iota(jnp.int32, (NB, NB), 0) == lax.broadcasted_iota(jnp.int32, (NB, NB), 1), damping, 0.0)
        m_ref[:, pl.ds(kb, NB)] = h_ref[:, pl.ds(kb, NB)] * inv_n
        m_ref[pl.ds(kb, NB), pl.ds(kb, NB)] += eye
    @pl.loop(0, K)
    def _(k):
        kb = pl.multiple_of(k * NB, NB)
        rows = [m_ref[pl.ds(pl.multiple_of(kb + 8 * g, 8), 8), pl.ds(kb, NB)] for g in range(NB // 8)]
        xt = factor_block(rows)
        for g in range(NB // 8):
            xt_ref[8 * g:8 * g + 8, :] = xt[g]
        xhi, xlo = split2(xt_ref[...])
        x3 = jnp.concatenate([xhi, xlo, xhi], axis=0)
        mhi, mlo = split2(m_ref[:, pl.ds(kb, NB)])
        m_ref[:, pl.ds(kb, NB)] = nn(jnp.concatenate([mhi, mhi, mlo], axis=1), x3)
        m_ref[pl.ds(kb, NB), pl.ds(kb, NB)] = xt_ref[...]
        phi, plo = split2(m_ref[:, pl.ds(kb, NB)])
        p3_ref[...] = jnp.concatenate([phi, phi, plo], axis=1)
        q3_ref[...] = jnp.concatenate([phi, plo, phi], axis=1)
        @pl.loop(k + 1, K)
        def _(j):
            jb = pl.multiple_of(j * NB, NB)
            m_ref[pl.ds(kb, NB), pl.ds(jb, NB)] = jnp.zeros((NB, NB), F32)
            m_ref[:, pl.ds(jb, NB)] -= nt(p3_ref[...], q3_ref[pl.ds(jb, NB), :])
    @pl.loop(0, K)
    def _(k):
        kb = pl.multiple_of(k * NB, NB)
        x = m_ref[:, pl.ds(kb, NB)]
        row = lax.broadcasted_iota(jnp.int32, (n, NB), 0)
        x = jnp.where(row < kb + NB, x, 0.0)
        hi, lo = split2(x)
        hi_ref[:, pl.ds(kb, NB)] = hi
        lo_ref[:, pl.ds(kb, NB)] = lo

def chol(gram, total, damping):
    n = gram.shape[0]
    vm = pl.BlockSpec(memory_space=pltpu.VMEM)
    return pl.pallas_call(
        functools.partial(chol_kernel, 1.0 / total, damping),
        out_shape=(jax.ShapeDtypeStruct((n, n), BF),) * 2,
        in_specs=[vm], out_specs=(vm, vm),
        scratch_shapes=[pltpu.VMEM((n, n), F32), pltpu.VMEM((NB, NB), F32),
                        pltpu.VMEM((n, 3 * NB), BF), pltpu.VMEM((n, 3 * NB), BF)],
        name="chol",
    )(gram)


def exchange(block, round_masks):
    first, second = block, block
    size = lax.axis_size("row")
    for bit in range(size.bit_length() - 1):
        use = jnp.bitwise_and(jnp.right_shift(round_masks[0], bit), 1) == 1
        moving = jnp.where(use, first, second)
        moved = lax.ppermute(moving, "row", [(i, i ^ 1 << bit) for i in range(size)])
        first = jnp.where(use, moved, first)
        second = jnp.where(use, second, moved)
    return first, second


def whiten(rows, inv_hi, inv_lo):
    return nn(jnp.concatenate([rows, rows], 1), jnp.concatenate([inv_hi, inv_lo], 0)).astype(BF)


def shards(grads, round_masks):
    row_count, width = grads.shape
    total = row_count * lax.axis_size("row") * lax.axis_size("col")
    gram = lax.dot_general(grads, grads, (((0,), (0,)), ((), ())), preferred_element_type=F32)
    sent, gram = lax.optimization_barrier((grads, gram))
    partners = exchange(sent, round_masks)
    gram = lax.psum(gram, ("row", "col"))
    inv_hi, inv_lo = chol(gram, total, DAMPING)
    white = whiten(grads, inv_hi, inv_lo)
    scale = 1.0 / (width ** 0.5)
    return jnp.stack([nt(white, whiten(p, inv_hi, inv_lo)) * scale for p in partners], axis=0)


def solution(mesh):
    return jax.shard_map(
        shards,
        mesh=mesh,
        in_specs=(P(("row", "col"), None), P()),
        out_specs=P(None, ("row", "col"), None),
        check_vma=False,
    )
```

```python
import functools
import jax, jax.numpy as jnp
from jax import lax
from jax.experimental import pallas as pl
from jax.experimental.pallas import tpu as pltpu
from jax.sharding import PartitionSpec as P

F32, BF = jnp.float32, jnp.bfloat16
NB = 128

DAMPING = 0.1
MESH = pl.DeviceIdType.MESH
NX, NY, NZ = 4, 4, 8
HOPS = 5
COPIES = 41
SCHEDULE = ((0, 0, 1), (2, 1, 1), (2, 0, 2), (4, 0, 3), (4, 1, 2), (6, 1, 3))


def recip(x):
    return 1.0 / x

def factor_block(rows):
    lane = lax.broadcasted_iota(jnp.int32, (8, 128), 1)
    sub = lax.broadcasted_iota(jnp.int32, (8, 128), 0)
    M = list(rows)
    drow = jnp.ones((8, 128), F32)
    G = len(M)
    for g in range(G):
        base = 8 * g
        R = M[g]
        r = [jnp.broadcast_to(R[a:a+1, :], (8, 128)) for a in range(8)]
        s = {(a, b): jnp.broadcast_to(r[a][:, base+b:base+b+1], (8, 128)) for a in range(8) for b in range(a, 8)}
        l = {}
        f = [None] * 8
        for a in range(8):
            i = recip(s[a, a])
            drow = jnp.where(lane == base + a, s[a, a], drow)
            for b in range(a + 1, 8):
                l[a, b] = s[a, b] * i
                r[b] = r[b] - l[a, b] * r[a]
                for c in range(b, 8):
                    s[b, c] = s[b, c] - l[a, b] * s[a, c]
            f[a] = jnp.where(lane > base + a, r[a] * i, 0.0)
        h = list(f)
        for a in range(6, -1, -1):
            for b in range(a + 1, 8):
                h[a] = h[a] - l[a, b] * h[b]
        order = list(range(g + 1, G)) + list(range(g))
        for v in order:
            c = [jnp.broadcast_to(M[v][:, base+a:base+a+1], (8, 128)) for a in range(8)]
            t = c[0] * h[0]
            for a in range(1, 8):
                t = t + c[a] * h[a]
            M[v] = M[v] - t
        acc = jnp.where(lane == base + sub, 1.0, 0.0)
        hh = h[0]
        for a in range(1, 8):
            hh = jnp.where(sub == a, h[a], hh)
        M[g] = acc - hh
    y = lax.rsqrt(drow)
    y = y * (1.5 - 0.5 * drow * y * y)
    return [m * y for m in M]

def split2(x):
    hi = x.astype(BF)
    lo = (x - hi.astype(F32)).astype(BF)
    return hi, lo

def nt(a, b):
    return lax.dot_general(a, b, (((1,), (1,)), ((), ())), preferred_element_type=F32)

def nn(a, b):
    return lax.dot_general(a, b, (((1,), (0,)), ((), ())), preferred_element_type=F32)


class Place:
    def __init__(self):
        self.row, self.col = lax.axis_index("row"), lax.axis_index("col")
        self.core = self.row % 2
        self.y = (self.row // 2) % NY
        self.x = self.col % NX
        self.z = (self.col // NX) * 4 + self.row // (2 * NY)

    def at(self, core=None, x=None, y=None, z=None):
        core = self.core if core is None else core
        x = self.x if x is None else x
        y = self.y if y is None else y
        z = self.z if z is None else z
        return (((z % 4) * NY + y) * 2 + core, (z // 4) * NX + x)

    def across(self, bit):
        w = 1 << bit
        return (self.row + (1 - 2 * ((self.row // w) % 2)) * w, self.col)


def tri(i, j):
    return i * (i + 1) // 2 + j


class Copies:
    def __init__(self, send_sems, recv_sems):
        self.send_sems, self.recv_sems, self.n, self.started = send_sems, recv_sems, 0, []

    def send(self, src, dst, device):
        c = pltpu.make_async_remote_copy(
            src_ref=src, dst_ref=dst, send_sem=self.send_sems.at[self.n], recv_sem=self.recv_sems.at[self.n],
            device_id=device, device_id_type=MESH)
        self.n += 1
        c.start()
        self.started.append(c)
        return c


def scatter(copies, src, base, piece, n, me, device_of, recv):
    out = []
    for d in range(1, n):
        p = (me + d) % n
        out.append(copies.send(src.at[pl.ds(pl.multiple_of(base + p * piece, 8), piece)], recv.at[d - 1], device_of(p)))
    return out


def gather(copies, buf, base, piece, n, me, device_of):
    out = []
    mine = buf.at[pl.ds(pl.multiple_of(base + me * piece, 8), piece)]
    for d in range(1, n):
        out.append(copies.send(mine, mine, device_of((me + d) % n)))
    return out


def arrived(cs):
    for c in cs:
        c.wait_recv()


def mega_kernel(inv_n, g_ref, mask_ref, hi_ref, lo_ref, part_ref,
                gram, rcore, ra1, t1, rb1, ra2, t2, rb2, u, rz, zb, red,
                m_ref, xt_ref, p3_ref, q3_ref, ab, xs, ys, send_sems, recv_sems, hop_sems):
    at = Place()
    copies = Copies(send_sems, recv_sems)
    barrier = pltpu.get_barrier_semaphore()
    others = [at.at(core=1 - at.core)]
    others += [at.at(x=(at.x + d) % NX) for d in range(1, NX)]
    others += [at.at(y=(at.y + d) % NY) for d in range(1, NY)]
    others += [at.at(z=(at.z + d) % NZ) for d in range(1, NZ)]
    for o in others:
        pl.semaphore_signal(barrier, inc=1, device_id=o, device_id_type=MESH)

    n = g_ref.shape[1]
    K = n // NB
    rows = g_ref.shape[0]
    half = rows // 2
    for i in range(K):
        b = lax.dot_general(g_ref[:, i * NB:(i + 1) * NB], g_ref[:, :(i + 1) * NB], (((0,), (0,)), ((), ())),
                            preferred_element_type=F32)
        for j in range(i + 1):
            gram[tri(i, j) * NB:(tri(i, j) + 1) * NB, :] = b[:, j * NB:(j + 1) * NB]
    pl.semaphore_wait(barrier, len(others))

    orders = ((0, 1, 2, 3, 4), (3, 4, 1, 2, 0))
    def hop(piece, h):
        src = g_ref.at[pl.ds(piece * half, half)] if h == 0 else xs.at[h - 1, piece]
        return pltpu.make_async_remote_copy(
            src_ref=src, dst_ref=ys.at[h, piece], send_sem=hop_sems.at[0, h, piece], recv_sem=hop_sems.at[1, h, piece],
            device_id=at.across(orders[piece][h]), device_id_type=MESH)

    def next_hop(piece, h):
        hop(piece, h).wait_recv()
        last = h == HOPS - 1
        bit, nbit = orders[piece][h], orders[piece][min(h + 1, HOPS - 1)]
        m, mn = mask_ref[bit * 16:bit * 16 + 16, :], mask_ref[nbit * 16:nbit * 16 + 16, :]

        @pl.loop(0, half // 16)
        def _(t):
            r = pl.ds(pl.multiple_of(t * 16, 16), 16)
            rr = pl.ds(pl.multiple_of(piece * half + t * 16, 16), 16)
            y = ys[h, piece, r, :]
            a = g_ref[rr, :] if h == 0 else ab[0, rr, :]
            b = g_ref[rr, :] if h == 0 else ab[1, rr, :]
            a2 = m * y + (1 - m) * a
            b2 = m * b + (1 - m) * y
            if last:
                part_ref[0, rr, :] = a2
                part_ref[1, rr, :] = b2
            else:
                ab[0, rr, :] = a2
                ab[1, rr, :] = b2
                xs[h, piece, r, :] = mn * a2 + (1 - mn) * b2
        if not last:
            hop(piece, h + 1).start()

    hr = gram.shape[0] // 2
    qr = hr // 2
    pa, pb = qr // 4, qr // 16
    pz = zb.shape[0] // NZ
    theirs = pl.multiple_of((1 - at.core) * hr, 8)
    ours = pl.multiple_of(at.core * hr, 8)
    c = copies.send(gram.at[pl.ds(theirs, hr)], rcore, at.at(core=1 - at.core))
    hop(0, 0).start()
    hop(1, 0).start()
    c.wait_recv()
    rcore[...] += gram[pl.ds(ours, hr), :]
    xdev, ydev, zdev = (lambda p: at.at(x=p)), (lambda p: at.at(y=p)), (lambda p: at.at(z=p))
    c1 = scatter(copies, rcore, 0, pa, NX, at.x, xdev, ra1)
    c2 = scatter(copies, rcore, qr, pa, NY, at.y, ydev, ra2)
    u[2 * pb:, :] = jnp.zeros((u.shape[0] - 2 * pb, NB), F32)
    next_hop(0, 0)
    arrived(c1)
    t1[...] = rcore[pl.ds(pl.multiple_of(at.x * pa, 8), pa), :] + ra1[0] + ra1[1] + ra1[2]
    c1 = scatter(copies, t1, 0, pb, NY, at.y, ydev, rb1)
    arrived(c2)
    t2[...] = rcore[pl.ds(pl.multiple_of(qr + at.y * pa, 8), pa), :] + ra2[0] + ra2[1] + ra2[2]
    c2 = scatter(copies, t2, 0, pb, NX, at.x, xdev, rb2)
    arrived(c1)
    u[:pb, :] = t1[pl.ds(pl.multiple_of(at.y * pb, 8), pb), :] + rb1[0] + rb1[1] + rb1[2]
    arrived(c2)
    u[pb:2 * pb, :] = t2[pl.ds(pl.multiple_of(at.x * pb, 8), pb), :] + rb2[0] + rb2[1] + rb2[2]
    c = scatter(copies, u, 0, pz, NZ, at.z, zdev, rz)
    arrived(c)
    mz = pl.ds(pl.multiple_of(at.z * pz, 8), pz)
    s = u[mz, :]
    for d in range(NZ - 1):
        s = s + rz[d]
    zb[mz, :] = s
    c = gather(copies, zb, 0, pz, NZ, at.z, zdev)
    arrived(c)
    b1 = ours + at.x * pa
    b2 = ours + qr + at.y * pa
    red[pl.ds(pl.multiple_of(b1 + at.y * pb, 8), pb), :] = zb[:pb, :]
    red[pl.ds(pl.multiple_of(b2 + at.x * pb, 8), pb), :] = zb[pb:2 * pb, :]
    c1 = gather(copies, red, b1, pb, NY, at.y, ydev)
    c2 = gather(copies, red, b2, pb, NX, at.x, xdev)
    arrived(c1)
    c1 = gather(copies, red, ours, pa, NX, at.x, xdev)
    arrived(c2)
    c2 = gather(copies, red, ours + qr, pa, NY, at.y, ydev)
    arrived(c1)
    r = red.at[pl.ds(ours, qr)]
    c1 = copies.send(r, r, at.at(core=1 - at.core))
    arrived(c2)
    r = red.at[pl.ds(pl.multiple_of(ours + qr, 8), qr)]
    c2 = copies.send(r, r, at.at(core=1 - at.core))
    next_hop(1, 0)
    arrived([c1, c2])

    eye = jnp.where(lax.broadcasted_iota(jnp.int32, (NB, NB), 0) == lax.broadcasted_iota(jnp.int32, (NB, NB), 1), DAMPING, 0.0)
    for i in range(K):
        for j in range(i + 1):
            b = red[tri(i, j) * NB:(tri(i, j) + 1) * NB, :] * inv_n
            m_ref[i * NB:(i + 1) * NB, j * NB:(j + 1) * NB] = b + eye if i == j else b

    @pl.loop(0, K)
    def _(k):
        for kk, piece, h in SCHEDULE:
            @pl.when(k == kk)
            def _():
                next_hop(piece, h)

        kb = pl.multiple_of(k * NB, NB)
        xt = factor_block([m_ref[pl.ds(pl.multiple_of(kb + 8 * g, 8), 8), pl.ds(kb, NB)] for g in range(NB // 8)])
        for g in range(NB // 8):
            xt_ref[8 * g:8 * g + 8, :] = xt[g]
        xhi, xlo = split2(xt_ref[...])
        x3 = jnp.concatenate([xhi, xlo, xhi], axis=0)
        mhi, mlo = split2(m_ref[:, pl.ds(kb, NB)])
        m_ref[:, pl.ds(kb, NB)] = nn(jnp.concatenate([mhi, mhi, mlo], axis=1), x3)
        m_ref[pl.ds(kb, NB), pl.ds(kb, NB)] = xt_ref[...]
        phi, plo = split2(m_ref[:, pl.ds(kb, NB)])
        p3_ref[...] = jnp.concatenate([phi, phi, plo], axis=1)
        q3_ref[...] = jnp.concatenate([phi, plo, phi], axis=1)

        @pl.loop(k + 1, K)
        def _(j):
            jb = pl.multiple_of(j * NB, NB)
            m_ref[pl.ds(kb, NB), pl.ds(jb, NB)] = jnp.zeros((NB, NB), F32)
            m_ref[:, pl.ds(jb, NB)] -= nt(p3_ref[...], q3_ref[pl.ds(jb, NB), :])

    next_hop(0, HOPS - 1)
    next_hop(1, HOPS - 1)

    @pl.loop(0, K)
    def _(k):
        kb = pl.multiple_of(k * NB, NB)
        x = m_ref[:, pl.ds(kb, NB)]
        x = jnp.where(lax.broadcasted_iota(jnp.int32, (n, NB), 0) < kb + NB, x, 0.0)
        hi, lo = split2(x)
        hi_ref[:, pl.ds(kb, NB)] = hi
        lo_ref[:, pl.ds(kb, NB)] = lo
    for c in copies.started:
        c.wait_send()
    for h in range(HOPS):
        hop(0, h).wait_send()
        hop(1, h).wait_send()


def mega(grads, masks, total):
    rows, n = grads.shape
    blocks = (n // NB) * (n // NB + 1) // 2
    tr = blocks * NB
    hr, qr = tr // 2, tr // 4
    pa, pb = qr // 4, qr // 16
    zr = -(-2 * pb // (8 * NZ)) * 8 * NZ
    half = rows // 2
    vm = pl.BlockSpec(memory_space=pltpu.VMEM)
    v = lambda *shape: pltpu.VMEM(shape, F32)
    b = lambda *shape: pltpu.VMEM(shape, BF)
    return pl.pallas_call(
        functools.partial(mega_kernel, 1.0 / total),
        out_shape=(jax.ShapeDtypeStruct((n, n), BF), jax.ShapeDtypeStruct((n, n), BF),
                   jax.ShapeDtypeStruct((2, rows, n), BF)),
        in_specs=[vm, vm], out_specs=(vm,) * 3,
        scratch_shapes=[v(tr, NB), v(hr, NB), v(3, pa, NB), v(pa, NB), v(3, pb, NB), v(3, pa, NB), v(pa, NB), v(3, pb, NB),
                        v(zr, NB), v(NZ - 1, zr // NZ, NB), v(zr, NB), v(tr, NB),
                        v(n, n), v(NB, NB), b(n, 3 * NB), b(n, 3 * NB), b(2, rows, n), b(HOPS - 1, 2, half, n), b(HOPS, 2, half, n),
                        pltpu.SemaphoreType.DMA((COPIES,)), pltpu.SemaphoreType.DMA((COPIES,)),
                        pltpu.SemaphoreType.DMA((2, HOPS, 2))],
        compiler_params=pltpu.CompilerParams(collective_id=0, has_side_effects=True, vmem_limit_bytes=60 * 2 ** 20),
        name="factor",
    )(grads, masks)


def whiten(rows, inv_hi, inv_lo):
    return nn(jnp.concatenate([rows, rows], 1), jnp.concatenate([inv_hi, inv_lo], 0)).astype(BF)


def shards(grads, round_masks):
    rows, width = grads.shape
    total = rows * lax.axis_size("row") * lax.axis_size("col")
    bits = jnp.bitwise_and(jnp.right_shift(round_masks[0], jnp.arange(HOPS)), 1).astype(BF)
    masks = jnp.broadcast_to(jnp.repeat(bits, 16)[:, None], (HOPS * 16, width))
    inv_hi, inv_lo, partners = mega(grads, masks, total)
    white = whiten(grads, inv_hi, inv_lo)
    scale = 1.0 / (width ** 0.5)
    return jnp.stack([nt(white, whiten(p, inv_hi, inv_lo)) * scale for p in (partners[0], partners[1])], axis=0)


def solution(mesh):
    return jax.shard_map(
        shards,
        mesh=mesh,
        in_specs=(P(("row", "col"), None), P()),
        out_specs=P(None, ("row", "col"), None),
        check_vma=False,
    )
```

```python
import functools
import jax, jax.numpy as jnp
from jax import lax
from jax.experimental import pallas as pl
from jax.experimental.pallas import tpu as pltpu
from jax.sharding import PartitionSpec as P

F32, BF = jnp.float32, jnp.bfloat16
NB = 128
WB = 256

DAMPING = 0.1
MESH = pl.DeviceIdType.MESH
NX, NY, NZ = 4, 4, 8
COPIES = 41
HOPS = 5
PIECES = 4
SCHEDULE = ((0, 0, 1), (1, 2, 1), (1, 3, 0), (2, 1, 1), (3, 0, 2), (3, 3, 1), (4, 2, 2), (5, 0, 3), (5, 1, 2),
            (6, 2, 3), (6, 3, 2), (6, 0, 4), (7, 1, 3))


def recip(x):
    return 1.0 / x

def factor_block(rows):
    lane = lax.broadcasted_iota(jnp.int32, (8, 128), 1)
    sub = lax.broadcasted_iota(jnp.int32, (8, 128), 0)
    M = list(rows)
    drow = jnp.ones((8, 128), F32)
    G = len(M)
    for g in range(G):
        base = 8 * g
        R = M[g]
        r = [jnp.broadcast_to(R[a:a+1, :], (8, 128)) for a in range(8)]
        s = {(a, b): jnp.broadcast_to(r[a][:, base+b:base+b+1], (8, 128)) for a in range(8) for b in range(a, 8)}
        l = {}
        f = [None] * 8
        for a in range(8):
            i = recip(s[a, a])
            drow = jnp.where(lane == base + a, s[a, a], drow)
            for b in range(a + 1, 8):
                l[a, b] = s[a, b] * i
                r[b] = r[b] - l[a, b] * r[a]
                for c in range(b, 8):
                    s[b, c] = s[b, c] - l[a, b] * s[a, c]
            f[a] = jnp.where(lane > base + a, r[a] * i, 0.0)
        h = list(f)
        for a in range(6, -1, -1):
            for b in range(a + 1, 8):
                h[a] = h[a] - l[a, b] * h[b]
        order = list(range(g + 1, G)) + list(range(g))
        for v in order:
            c = [jnp.broadcast_to(M[v][:, base+a:base+a+1], (8, 128)) for a in range(8)]
            t = c[0] * h[0]
            for a in range(1, 8):
                t = t + c[a] * h[a]
            M[v] = M[v] - t
        acc = jnp.where(lane == base + sub, 1.0, 0.0)
        hh = h[0]
        for a in range(1, 8):
            hh = jnp.where(sub == a, h[a], hh)
        M[g] = acc - hh
    y = lax.rsqrt(drow)
    y = y * (1.5 - 0.5 * drow * y * y)
    return [m * y for m in M]

def split2(x):
    hi = x.astype(BF)
    lo = (x - hi.astype(F32)).astype(BF)
    return hi, lo

def nt(a, b):
    return lax.dot_general(a, b, (((1,), (1,)), ((), ())), preferred_element_type=F32)

def nn(a, b):
    return lax.dot_general(a, b, (((1,), (0,)), ((), ())), preferred_element_type=F32)


class Place:
    def __init__(self):
        self.row, self.col = lax.axis_index("row"), lax.axis_index("col")
        self.core = self.row % 2
        self.y = (self.row // 2) % NY
        self.x = self.col % NX
        self.z = (self.col // NX) * 4 + self.row // (2 * NY)

    def at(self, core=None, x=None, y=None, z=None):
        core = self.core if core is None else core
        x = self.x if x is None else x
        y = self.y if y is None else y
        z = self.z if z is None else z
        return (((z % 4) * NY + y) * 2 + core, (z // 4) * NX + x)

    def across(self, bit):
        w = 1 << bit
        return (self.row + (1 - 2 * ((self.row // w) % 2)) * w, self.col)


def tri(i, j):
    return i * (i + 1) // 2 + j


class Copies:
    def __init__(self, send_sems, recv_sems):
        self.send_sems, self.recv_sems, self.n, self.started = send_sems, recv_sems, 0, []

    def send(self, src, dst, device):
        c = pltpu.make_async_remote_copy(
            src_ref=src, dst_ref=dst, send_sem=self.send_sems.at[self.n], recv_sem=self.recv_sems.at[self.n],
            device_id=device, device_id_type=MESH)
        self.n += 1
        c.start()
        self.started.append(c)
        return c


def scatter(copies, src, base, piece, n, me, device_of, recv):
    out = []
    for d in range(1, n):
        p = (me + d) % n
        out.append(copies.send(src.at[pl.ds(pl.multiple_of(base + p * piece, 8), piece)], recv.at[d - 1], device_of(p)))
    return out


def gather(copies, buf, base, piece, n, me, device_of):
    out = []
    mine = buf.at[pl.ds(pl.multiple_of(base + me * piece, 8), piece)]
    for d in range(1, n):
        out.append(copies.send(mine, mine, device_of((me + d) % n)))
    return out


def arrived(cs):
    for c in cs:
        c.wait_recv()


def mega_kernel(inv_n, g_ref, mask_ref, out_ref,
                gram, rcore, ra1, t1, rb1, ra2, t2, rb2, u, rz, zb, red,
                m_ref, xt_ref, p3_ref, q3_ref, hi_ref, lo_ref, kept, kept2, xs, ys, ys2, partners, own, other, send_sems, recv_sems, hop_sems):
    at = Place()
    copies = Copies(send_sems, recv_sems)
    barrier = pltpu.get_barrier_semaphore()
    others = [at.at(core=1 - at.core)]
    others += [at.at(x=(at.x + d) % NX) for d in range(1, NX)]
    others += [at.at(y=(at.y + d) % NY) for d in range(1, NY)]
    others += [at.at(z=(at.z + d) % NZ) for d in range(1, NZ)]
    for o in others:
        pl.semaphore_signal(barrier, inc=1, device_id=o, device_id_type=MESH)

    n = g_ref.shape[1]
    K = n // NB
    rows = g_ref.shape[0]
    part = rows // PIECES
    across = [at.across(bit) for bit in range(HOPS)]
    mirror = at.at(y=NY - 1 - at.y)
    routes = ((across[4], across[3], across[1], mirror, across[0]), (across[1], mirror, across[4], across[3], across[0]))
    flags = ((0, None, None, 3, 4), (1, 5, 0, 6, 4))

    def hop(piece, h, second=False):
        y_first = piece // 2
        if h == 0:
            src = g_ref.at[pl.ds(piece * part, part)]
        elif h == 2 and not y_first:
            src = ys.at[1, piece] if second else kept.at[pl.ds(piece * part, part)]
        else:
            src = xs.at[h - 1, piece]
        return pltpu.make_async_remote_copy(
            src_ref=src, dst_ref=ys2.at[piece] if second else ys.at[h, piece],
            send_sem=hop_sems.at[0, HOPS if second else h, piece], recv_sem=hop_sems.at[1, HOPS if second else h, piece],
            device_id=routes[y_first][h], device_id_type=MESH)

    def pick(flag, a, b):
        m = mask_ref[flag * 16:flag * 16 + 16, :]
        return m * a + (1 - m) * b, m * b + (1 - m) * a

    def next_hop(piece, h):
        y_first = piece // 2
        hop(piece, h).wait_recv()
        if h == 1 and not y_first:
            hop(piece, 2).start()
            hop(piece, 2, True).start()
            return
        if h == 2 and not y_first:
            hop(piece, 2, True).wait_recv()

        @pl.loop(0, part // 16)
        def _(t):
            r = pl.ds(pl.multiple_of(t * 16, 16), 16)
            rr = pl.ds(pl.multiple_of(piece * part + t * 16, 16), 16)
            y = ys[h, piece, r, :]
            if h == 0:
                p = g_ref[rr, :]
            elif y_first:
                p = xs[0, piece, r, :] if h == 1 else kept[rr, :]
            else:
                p = kept[rr, :] if h == 2 else kept2[rr, :]
            if h == 2 and not y_first:
                p = pick(1, y, p)[0]
                y = pick(1, ys2[piece, r, :], ys[1, piece, r, :])[0]
                go, stay = pick(2, y, p)
            else:
                go, stay = pick(flags[y_first][h], y, p)
            if h == HOPS - 1:
                partners[0, rr, :] = go
                partners[1, rr, :] = stay
            else:
                xs[h, piece, r, :] = go
                if y_first or h == 0:
                    kept[rr, :] = stay
                else:
                    kept2[rr, :] = stay
        if h < HOPS - 1:
            hop(piece, h + 1).start()

    for i in range(K):
        if i == K // 2:
            pl.semaphore_wait(barrier, len(others))
            hop(0, 0).start()
            hop(1, 0).start()
        b = lax.dot_general(g_ref[:, i * NB:(i + 1) * NB], g_ref[:, :(i + 1) * NB], (((0,), (0,)), ((), ())),
                            preferred_element_type=F32)
        for j in range(i + 1):
            gram[tri(i, j) * NB:(tri(i, j) + 1) * NB, :] = b[:, j * NB:(j + 1) * NB]

    hr = gram.shape[0] // 2
    qr = hr // 2
    pa, pb = qr // 4, qr // 16
    pz = zb.shape[0] // NZ
    theirs = pl.multiple_of((1 - at.core) * hr, 8)
    ours = pl.multiple_of(at.core * hr, 8)
    c = copies.send(gram.at[pl.ds(theirs, hr)], rcore, at.at(core=1 - at.core))
    c.wait_recv()
    rcore[...] += gram[pl.ds(ours, hr), :]
    xdev, ydev, zdev = (lambda p: at.at(x=p)), (lambda p: at.at(y=p)), (lambda p: at.at(z=p))
    c1 = scatter(copies, rcore, 0, pa, NX, at.x, xdev, ra1)
    c2 = scatter(copies, rcore, qr, pa, NY, at.y, ydev, ra2)
    u[2 * pb:, :] = jnp.zeros((u.shape[0] - 2 * pb, NB), F32)
    arrived(c1)
    t1[...] = rcore[pl.ds(pl.multiple_of(at.x * pa, 8), pa), :] + ra1[0] + ra1[1] + ra1[2]
    c1 = scatter(copies, t1, 0, pb, NY, at.y, ydev, rb1)
    arrived(c2)
    t2[...] = rcore[pl.ds(pl.multiple_of(qr + at.y * pa, 8), pa), :] + ra2[0] + ra2[1] + ra2[2]
    c2 = scatter(copies, t2, 0, pb, NX, at.x, xdev, rb2)
    arrived(c1)
    u[:pb, :] = t1[pl.ds(pl.multiple_of(at.y * pb, 8), pb), :] + rb1[0] + rb1[1] + rb1[2]
    arrived(c2)
    u[pb:2 * pb, :] = t2[pl.ds(pl.multiple_of(at.x * pb, 8), pb), :] + rb2[0] + rb2[1] + rb2[2]
    c = scatter(copies, u, 0, pz, NZ, at.z, zdev, rz)
    hop(2, 0).start()
    arrived(c)
    mz = pl.ds(pl.multiple_of(at.z * pz, 8), pz)
    s = u[mz, :]
    for d in range(NZ - 1):
        s = s + rz[d]
    zb[mz, :] = s
    c = gather(copies, zb, 0, pz, NZ, at.z, zdev)
    arrived(c)
    next_hop(0, 0)
    next_hop(1, 0)
    b1 = ours + at.x * pa
    b2 = ours + qr + at.y * pa
    red[pl.ds(pl.multiple_of(b1 + at.y * pb, 8), pb), :] = zb[:pb, :]
    red[pl.ds(pl.multiple_of(b2 + at.x * pb, 8), pb), :] = zb[pb:2 * pb, :]
    c1 = gather(copies, red, b1, pb, NY, at.y, ydev)
    c2 = gather(copies, red, b2, pb, NX, at.x, xdev)
    arrived(c1)
    c1 = gather(copies, red, ours, pa, NX, at.x, xdev)
    arrived(c2)
    c2 = gather(copies, red, ours + qr, pa, NY, at.y, ydev)
    arrived(c1)
    r = red.at[pl.ds(ours, qr)]
    c1 = copies.send(r, r, at.at(core=1 - at.core))
    arrived(c2)
    r = red.at[pl.ds(pl.multiple_of(ours + qr, 8), qr)]
    c2 = copies.send(r, r, at.at(core=1 - at.core))
    hop(3, 0).start()
    next_hop(2, 0)
    arrived([c1, c2])

    eye = jnp.where(lax.broadcasted_iota(jnp.int32, (NB, NB), 0) == lax.broadcasted_iota(jnp.int32, (NB, NB), 1), DAMPING, 0.0)
    for i in range(K):
        for j in range(i + 1):
            b = red[tri(i, j) * NB:(tri(i, j) + 1) * NB, :] * inv_n
            m_ref[i * NB:(i + 1) * NB, j * NB:(j + 1) * NB] = b + eye if i == j else b

    p3_ref[...] = jnp.zeros_like(p3_ref)
    q3_ref[...] = jnp.zeros_like(q3_ref)
    col = lax.broadcasted_iota(jnp.int32, (NB, n), 1)
    prow = lax.broadcasted_iota(jnp.int32, (n, NB), 0)
    qrow = lax.broadcasted_iota(jnp.int32, (n, 3 * NB), 0)

    @pl.loop(0, K)
    def _(k):
        for kk, piece, h in SCHEDULE:
            @pl.when(k == kk)
            def _():
                next_hop(piece, h)

        kb = pl.multiple_of(k * NB, NB)
        block = [m_ref[pl.ds(pl.multiple_of(kb + 8 * g, 8), 8), pl.ds(kb, NB)] for g in range(NB // 8)]
        for c in range(0, n, WB):
            m_ref[:, c:c + WB] -= nt(p3_ref[...], q3_ref[c:c + WB, :])
        xt = factor_block(block)
        for g in range(NB // 8):
            xt_ref[8 * g:8 * g + 8, :] = xt[g]
        xhi, xlo = split2(xt_ref[...])
        x3 = jnp.concatenate([xhi, xlo, xhi], axis=0)
        mhi, mlo = split2(m_ref[:, pl.ds(kb, NB)])
        m_ref[:, pl.ds(kb, NB)] = nn(jnp.concatenate([mhi, mhi, mlo], axis=1), x3)
        m_ref[pl.ds(kb, NB), pl.ds(kb, NB)] = xt_ref[...]
        m_ref[pl.ds(kb, NB), :] = jnp.where(col < kb + NB, m_ref[pl.ds(kb, NB), :], 0.0)
        phi, plo = split2(m_ref[:, pl.ds(kb, NB)])
        zero = jnp.zeros_like(phi)
        hi_ref[:, pl.ds(kb, NB)] = jnp.where(prow < kb + NB, phi, zero)
        lo_ref[:, pl.ds(kb, NB)] = jnp.where(prow < kb + NB, plo, zero)
        p3_ref[...] = jnp.concatenate([phi, phi, plo], axis=1)
        q3_ref[...] = jnp.concatenate([phi, plo, phi], axis=1)

        @pl.when(k + 1 < K)
        def _():
            jb = pl.multiple_of(kb + NB, NB)
            m_ref[:, pl.ds(jb, NB)] -= nt(p3_ref[...], q3_ref[pl.ds(jb, NB), :])

        q3_ref[...] = jnp.where(qrow < kb + 2 * NB, jnp.zeros_like(q3_ref), q3_ref[...])

    def whiten(src, dst):
        for c in range(0, n, WB):
            e = c + WB
            r = src[:, :e]
            dst[:, c:e] = (nn(r, hi_ref[:e, c:e]) + nn(r, lo_ref[:e, c:e])).astype(BF)

    next_hop(3, HOPS - 2)
    next_hop(1, HOPS - 1)
    next_hop(2, HOPS - 1)
    whiten(g_ref, own)
    next_hop(3, HOPS - 1)
    for r in range(2):
        whiten(partners.at[r], other.at[r])
        out_ref[r] = nt(own[...], other[r]) * (1.0 / n ** 0.5)
    for c in copies.started:
        c.wait_send()
    for h in range(HOPS):
        for p in range(PIECES):
            hop(p, h).wait_send()
    hop(0, 2, True).wait_send()
    hop(1, 2, True).wait_send()


def mega(grads, masks, total):
    rows, n = grads.shape
    blocks = (n // NB) * (n // NB + 1) // 2
    tr = blocks * NB
    hr, qr = tr // 2, tr // 4
    pa, pb = qr // 4, qr // 16
    zr = -(-2 * pb // (8 * NZ)) * 8 * NZ
    part = rows // PIECES
    vm = pl.BlockSpec(memory_space=pltpu.VMEM)
    v = lambda *shape: pltpu.VMEM(shape, F32)
    b = lambda *shape: pltpu.VMEM(shape, BF)
    return pl.pallas_call(
        functools.partial(mega_kernel, 1.0 / total),
        out_shape=jax.ShapeDtypeStruct((2, rows, rows), F32),
        in_specs=[vm, vm], out_specs=vm,
        scratch_shapes=[v(tr, NB), v(hr, NB), v(3, pa, NB), v(pa, NB), v(3, pb, NB), v(3, pa, NB), v(pa, NB), v(3, pb, NB),
                        v(zr, NB), v(NZ - 1, zr // NZ, NB), v(zr, NB), v(tr, NB),
                        v(n, n), v(NB, NB), b(n, 3 * NB), b(n, 3 * NB), b(n, n), b(n, n),
                        b(rows, n), b(rows, n), b(HOPS - 1, PIECES, part, n), b(HOPS, PIECES, part, n), b(2, part, n),
                        b(2, rows, n), b(rows, n), b(2, rows, n),
                        pltpu.SemaphoreType.DMA((COPIES,)), pltpu.SemaphoreType.DMA((COPIES,)),
                        pltpu.SemaphoreType.DMA((2, HOPS + 1, PIECES))],
        compiler_params=pltpu.CompilerParams(collective_id=0, has_side_effects=True, vmem_limit_bytes=60 * 2 ** 20),
        name="factor",
    )(grads, masks)


def shards(grads, round_masks):
    rows, width = grads.shape
    total = rows * lax.axis_size("row") * lax.axis_size("col")
    bit = [jnp.bitwise_and(jnp.right_shift(round_masks[0], b), 1) for b in range(HOPS)]
    flags = jnp.stack([bit[3] == bit[4], bit[1] != bit[2], bit[2] == bit[3], bit[0] == bit[2], bit[0] == 1,
                       bit[4] == bit[2], bit[0] == bit[3]]).astype(BF)
    masks = jnp.broadcast_to(jnp.repeat(flags, 16)[:, None], (flags.shape[0] * 16, width))
    return mega(grads, masks, total)


def solution(mesh):
    return jax.shard_map(
        shards,
        mesh=mesh,
        in_specs=(P(("row", "col"), None), P()),
        out_specs=P(None, ("row", "col"), None),
        check_vma=False,
    )
```

```python
import functools
import jax, jax.numpy as jnp
from jax import lax
from jax.experimental import pallas as pl
from jax.experimental.pallas import tpu as pltpu
from jax.sharding import PartitionSpec as P

F32, BF = jnp.float32, jnp.bfloat16
NB = 128
WB = 256

DAMPING = 0.1
MESH = pl.DeviceIdType.MESH
NX, NY, NZ = 4, 4, 8
COPIES = 41
HOPS = 5
PIECES = 4
SCHEDULE = ((1, 0, 1), (1, 3, 0), (2, 2, 1), (2, 1, 1), (3, 3, 1), (4, 0, 2), (5, 2, 2), (6, 0, 3), (6, 1, 2),
            (7, 2, 3), (7, 3, 2), (7, 0, 4))


def recip(x):
    return 1.0 / x

def factor_block(rows):
    lane = lax.broadcasted_iota(jnp.int32, (8, 128), 1)
    sub = lax.broadcasted_iota(jnp.int32, (8, 128), 0)
    M = list(rows)
    drow = jnp.ones((8, 128), F32)
    G = len(M)
    for g in range(G):
        base = 8 * g
        R = M[g]
        r = [jnp.broadcast_to(R[a:a+1, :], (8, 128)) for a in range(8)]
        s = {(a, b): jnp.broadcast_to(r[a][:, base+b:base+b+1], (8, 128)) for a in range(8) for b in range(a, 8)}
        l = {}
        f = [None] * 8
        for a in range(8):
            i = recip(s[a, a])
            drow = jnp.where(lane == base + a, s[a, a], drow)
            for b in range(a + 1, 8):
                l[a, b] = s[a, b] * i
                r[b] = r[b] - l[a, b] * r[a]
                for c in range(b, 8):
                    s[b, c] = s[b, c] - l[a, b] * s[a, c]
            f[a] = jnp.where(lane > base + a, r[a] * i, 0.0)
        h = list(f)
        for a in range(6, -1, -1):
            for b in range(a + 1, 8):
                h[a] = h[a] - l[a, b] * h[b]
        order = list(range(g + 1, G)) + list(range(g))
        for v in order:
            c = [jnp.broadcast_to(M[v][:, base+a:base+a+1], (8, 128)) for a in range(8)]
            t = c[0] * h[0]
            for a in range(1, 8):
                t = t + c[a] * h[a]
            M[v] = M[v] - t
        acc = jnp.where(lane == base + sub, 1.0, 0.0)
        hh = h[0]
        for a in range(1, 8):
            hh = jnp.where(sub == a, h[a], hh)
        M[g] = acc - hh
    y = lax.rsqrt(drow)
    y = y * (1.5 - 0.5 * drow * y * y)
    return [m * y for m in M]

def split2(x):
    hi = x.astype(BF)
    lo = (x - hi.astype(F32)).astype(BF)
    return hi, lo

def nt(a, b):
    return lax.dot_general(a, b, (((1,), (1,)), ((), ())), preferred_element_type=F32)

def nn(a, b):
    return lax.dot_general(a, b, (((1,), (0,)), ((), ())), preferred_element_type=F32)


class Place:
    def __init__(self):
        self.row, self.col = lax.axis_index("row"), lax.axis_index("col")
        self.core = self.row % 2
        self.y = (self.row // 2) % NY
        self.x = self.col % NX
        self.z = (self.col // NX) * 4 + self.row // (2 * NY)

    def at(self, core=None, x=None, y=None, z=None):
        core = self.core if core is None else core
        x = self.x if x is None else x
        y = self.y if y is None else y
        z = self.z if z is None else z
        return (((z % 4) * NY + y) * 2 + core, (z // 4) * NX + x)

    def across(self, bit):
        w = 1 << bit
        return (self.row + (1 - 2 * ((self.row // w) % 2)) * w, self.col)


def tri(i, j):
    return i * (i + 1) // 2 + j


class Copies:
    def __init__(self, send_sems, recv_sems):
        self.send_sems, self.recv_sems, self.n, self.started = send_sems, recv_sems, 0, []

    def send(self, src, dst, device):
        c = pltpu.make_async_remote_copy(
            src_ref=src, dst_ref=dst, send_sem=self.send_sems.at[self.n], recv_sem=self.recv_sems.at[self.n],
            device_id=device, device_id_type=MESH)
        self.n += 1
        c.start()
        self.started.append(c)
        return c


def scatter(copies, src, base, piece, n, me, device_of, recv):
    out = []
    for d in range(1, n):
        p = (me + d) % n
        out.append(copies.send(src.at[pl.ds(pl.multiple_of(base + p * piece, 8), piece)], recv.at[d - 1], device_of(p)))
    return out


def gather(copies, buf, base, piece, n, me, device_of):
    out = []
    mine = buf.at[pl.ds(pl.multiple_of(base + me * piece, 8), piece)]
    for d in range(1, n):
        out.append(copies.send(mine, mine, device_of((me + d) % n)))
    return out


def arrived(cs):
    for c in cs:
        c.wait_recv()


def mega_kernel(inv_n, g_ref, mask_ref, out_ref,
                gram, rcore, ra1, t1, rb1, ra2, t2, rb2, u, rz, zb, red,
                m_ref, xt_ref, p3_ref, q3_ref, hi_ref, lo_ref, kept, kept2, xs, ys, ys2, partners, own, other, send_sems, recv_sems, hop_sems):
    at = Place()
    copies = Copies(send_sems, recv_sems)
    barrier = pltpu.get_barrier_semaphore()
    others = [at.at(core=1 - at.core)]
    others += [at.at(x=(at.x + d) % NX) for d in range(1, NX)]
    others += [at.at(y=(at.y + d) % NY) for d in range(1, NY)]
    others += [at.at(z=(at.z + d) % NZ) for d in range(1, NZ)]
    for o in others:
        pl.semaphore_signal(barrier, inc=1, device_id=o, device_id_type=MESH)

    n = g_ref.shape[1]
    K = n // NB
    rows = g_ref.shape[0]
    part = rows // PIECES
    across = [at.across(bit) for bit in range(HOPS)]
    mirror = at.at(y=NY - 1 - at.y)
    routes = ((across[4], across[3], across[1], mirror, across[0]), (across[1], mirror, across[4], across[3], across[0]))
    flags = ((0, None, None, 3, 4), (1, 5, 0, 6, 4))

    def hop(piece, h, second=False):
        y_first = piece // 2
        if h == 0:
            src = g_ref.at[pl.ds(piece * part, part)]
        elif h == 2 and not y_first:
            src = ys.at[1, piece] if second else kept.at[pl.ds(piece * part, part)]
        else:
            src = xs.at[h - 1, piece]
        return pltpu.make_async_remote_copy(
            src_ref=src, dst_ref=ys2.at[piece] if second else ys.at[h, piece],
            send_sem=hop_sems.at[0, HOPS if second else h, piece], recv_sem=hop_sems.at[1, HOPS if second else h, piece],
            device_id=routes[y_first][h], device_id_type=MESH)

    def flag(f):
        m = mask_ref[f * 16:f * 16 + 16, :]
        return m, 1 - m

    def pick(f, a, b):
        return f[0] * a + f[1] * b, f[0] * b + f[1] * a

    def next_hop(piece, h):
        y_first = piece // 2
        hop(piece, h).wait_recv()
        if h == 1 and not y_first:
            hop(piece, 2).start()
            hop(piece, 2, True).start()
            return
        if h == 2 and not y_first:
            hop(piece, 2, True).wait_recv()

        both = h == 2 and not y_first
        f = flag(2 if both else flags[y_first][h])
        f1 = flag(1) if both else None

        def rows16(base):
            r = pl.ds(pl.multiple_of(base, 16), 16)
            rr = pl.ds(pl.multiple_of(piece * part + base, 16), 16)
            y = ys[h, piece, r, :]
            if h == 0:
                p = g_ref[rr, :]
            elif y_first:
                p = xs[0, piece, r, :] if h == 1 else kept[rr, :]
            else:
                p = kept[rr, :] if h == 2 else kept2[rr, :]
            if both:
                p = pick(f1, y, p)[0]
                y = pick(f1, ys2[piece, r, :], ys[1, piece, r, :])[0]
            go, stay = pick(f, y, p)
            if h == HOPS - 1:
                partners[0, rr, :] = go
                partners[1, rr, :] = stay
            else:
                xs[h, piece, r, :] = go
                if y_first or h == 0:
                    kept[rr, :] = stay
                else:
                    kept2[rr, :] = stay

        @pl.loop(0, 2)
        def _(t):
            for i in range(part // 32):
                rows16(t * (part // 2) + 16 * i)

        if h < HOPS - 1:
            hop(piece, h + 1).start()

    for i in range(K):
        if i == K // 2:
            pl.semaphore_wait(barrier, len(others))
            hop(0, 0).start()
        b = lax.dot_general(g_ref[:, i * NB:(i + 1) * NB], g_ref[:, :(i + 1) * NB], (((0,), (0,)), ((), ())),
                            preferred_element_type=F32)
        for j in range(i + 1):
            gram[tri(i, j) * NB:(tri(i, j) + 1) * NB, :] = b[:, j * NB:(j + 1) * NB]

    hr = gram.shape[0] // 2
    qr = hr // 2
    pa, pb = qr // 4, qr // 16
    pz = zb.shape[0] // NZ
    theirs = pl.multiple_of((1 - at.core) * hr, 8)
    ours = pl.multiple_of(at.core * hr, 8)
    c = copies.send(gram.at[pl.ds(theirs, hr)], rcore, at.at(core=1 - at.core))
    c.wait_recv()
    rcore[...] += gram[pl.ds(ours, hr), :]
    xdev, ydev, zdev = (lambda p: at.at(x=p)), (lambda p: at.at(y=p)), (lambda p: at.at(z=p))
    c1 = scatter(copies, rcore, 0, pa, NX, at.x, xdev, ra1)
    c2 = scatter(copies, rcore, qr, pa, NY, at.y, ydev, ra2)
    u[2 * pb:, :] = jnp.zeros((u.shape[0] - 2 * pb, NB), F32)
    arrived(c1)
    t1[...] = rcore[pl.ds(pl.multiple_of(at.x * pa, 8), pa), :] + ra1[0] + ra1[1] + ra1[2]
    c1 = scatter(copies, t1, 0, pb, NY, at.y, ydev, rb1)
    arrived(c2)
    t2[...] = rcore[pl.ds(pl.multiple_of(qr + at.y * pa, 8), pa), :] + ra2[0] + ra2[1] + ra2[2]
    c2 = scatter(copies, t2, 0, pb, NX, at.x, xdev, rb2)
    arrived(c1)
    u[:pb, :] = t1[pl.ds(pl.multiple_of(at.y * pb, 8), pb), :] + rb1[0] + rb1[1] + rb1[2]
    arrived(c2)
    u[pb:2 * pb, :] = t2[pl.ds(pl.multiple_of(at.x * pb, 8), pb), :] + rb2[0] + rb2[1] + rb2[2]
    c = scatter(copies, u, 0, pz, NZ, at.z, zdev, rz)
    hop(2, 0).start()
    arrived(c)
    mz = pl.ds(pl.multiple_of(at.z * pz, 8), pz)
    s = u[mz, :]
    for d in range(NZ - 1):
        s = s + rz[d]
    zb[mz, :] = s
    c = gather(copies, zb, 0, pz, NZ, at.z, zdev)
    arrived(c)
    hop(1, 0).start()
    next_hop(0, 0)
    b1 = ours + at.x * pa
    b2 = ours + qr + at.y * pa
    red[pl.ds(pl.multiple_of(b1 + at.y * pb, 8), pb), :] = zb[:pb, :]
    red[pl.ds(pl.multiple_of(b2 + at.x * pb, 8), pb), :] = zb[pb:2 * pb, :]
    c1 = gather(copies, red, b1, pb, NY, at.y, ydev)
    c2 = gather(copies, red, b2, pb, NX, at.x, xdev)
    arrived(c1)
    c1 = gather(copies, red, ours, pa, NX, at.x, xdev)
    arrived(c2)
    c2 = gather(copies, red, ours + qr, pa, NY, at.y, ydev)
    arrived(c1)
    r = red.at[pl.ds(ours, qr)]
    c1 = copies.send(r, r, at.at(core=1 - at.core))
    arrived(c2)
    r = red.at[pl.ds(pl.multiple_of(ours + qr, 8), qr)]
    c2 = copies.send(r, r, at.at(core=1 - at.core))
    hop(3, 0).start()
    next_hop(2, 0)
    arrived([c1, c2])
    next_hop(1, 0)

    eye = jnp.where(lax.broadcasted_iota(jnp.int32, (NB, NB), 0) == lax.broadcasted_iota(jnp.int32, (NB, NB), 1), DAMPING, 0.0)
    for i in range(K):
        for j in range(i + 1):
            b = red[tri(i, j) * NB:(tri(i, j) + 1) * NB, :] * inv_n
            m_ref[i * NB:(i + 1) * NB, j * NB:(j + 1) * NB] = b + eye if i == j else b

    p3_ref[...] = jnp.zeros_like(p3_ref)
    q3_ref[...] = jnp.zeros_like(q3_ref)
    col = lax.broadcasted_iota(jnp.int32, (NB, n), 1)
    prow = lax.broadcasted_iota(jnp.int32, (n, NB), 0)
    qrow = lax.broadcasted_iota(jnp.int32, (n, 3 * NB), 0)

    @pl.loop(0, K)
    def _(k):
        for kk, piece, h in SCHEDULE:
            @pl.when(k == kk)
            def _():
                next_hop(piece, h)

        kb = pl.multiple_of(k * NB, NB)
        block = [m_ref[pl.ds(pl.multiple_of(kb + 8 * g, 8), 8), pl.ds(kb, NB)] for g in range(NB // 8)]
        for c in range(0, n, WB):
            m_ref[:, c:c + WB] -= nt(p3_ref[...], q3_ref[c:c + WB, :])
        xt = factor_block(block)
        for g in range(NB // 8):
            xt_ref[8 * g:8 * g + 8, :] = xt[g]
        xhi, xlo = split2(xt_ref[...])
        x3 = jnp.concatenate([xhi, xlo, xhi], axis=0)
        mhi, mlo = split2(m_ref[:, pl.ds(kb, NB)])
        m_ref[:, pl.ds(kb, NB)] = nn(jnp.concatenate([mhi, mhi, mlo], axis=1), x3)
        m_ref[pl.ds(kb, NB), pl.ds(kb, NB)] = xt_ref[...]
        m_ref[pl.ds(kb, NB), :] = jnp.where(col < kb + NB, m_ref[pl.ds(kb, NB), :], 0.0)
        phi, plo = split2(m_ref[:, pl.ds(kb, NB)])
        zero = jnp.zeros_like(phi)
        hi_ref[:, pl.ds(kb, NB)] = jnp.where(prow < kb + NB, phi, zero)
        lo_ref[:, pl.ds(kb, NB)] = jnp.where(prow < kb + NB, plo, zero)
        p3_ref[...] = jnp.concatenate([phi, phi, plo], axis=1)
        q3_ref[...] = jnp.concatenate([phi, plo, phi], axis=1)

        @pl.when(k + 1 < K)
        def _():
            jb = pl.multiple_of(kb + NB, NB)
            m_ref[:, pl.ds(jb, NB)] -= nt(p3_ref[...], q3_ref[pl.ds(jb, NB), :])

        q3_ref[...] = jnp.where(qrow < kb + 2 * NB, jnp.zeros_like(q3_ref), q3_ref[...])

    def whiten(src, dst, first=0, end=n):
        for c in range(first, end, WB):
            e = c + WB
            r = src[:, :e]
            dst[:, c:e] = (nn(r, hi_ref[:e, c:e]) + nn(r, lo_ref[:e, c:e])).astype(BF)

    next_hop(1, HOPS - 2)
    whiten(g_ref, own, 0, n - WB)
    next_hop(3, HOPS - 2)
    next_hop(2, HOPS - 1)
    next_hop(1, HOPS - 1)
    whiten(g_ref, own, n - WB)
    next_hop(3, HOPS - 1)
    for r in range(2):
        whiten(partners.at[r], other.at[r])
        out_ref[r] = nt(own[...], other[r])
    for c in copies.started:
        c.wait_send()
    for h in range(HOPS):
        for p in range(PIECES):
            hop(p, h).wait_send()
    hop(0, 2, True).wait_send()
    hop(1, 2, True).wait_send()


def mega(grads, masks, total):
    rows, n = grads.shape
    blocks = (n // NB) * (n // NB + 1) // 2
    tr = blocks * NB
    hr, qr = tr // 2, tr // 4
    pa, pb = qr // 4, qr // 16
    zr = -(-2 * pb // (8 * NZ)) * 8 * NZ
    part = rows // PIECES
    vm = pl.BlockSpec(memory_space=pltpu.VMEM)
    v = lambda *shape: pltpu.VMEM(shape, F32)
    b = lambda *shape: pltpu.VMEM(shape, BF)
    return pl.pallas_call(
        functools.partial(mega_kernel, 1.0 / total),
        out_shape=jax.ShapeDtypeStruct((2, rows, rows), F32),
        in_specs=[vm, vm], out_specs=vm,
        scratch_shapes=[v(tr, NB), v(hr, NB), v(3, pa, NB), v(pa, NB), v(3, pb, NB), v(3, pa, NB), v(pa, NB), v(3, pb, NB),
                        v(zr, NB), v(NZ - 1, zr // NZ, NB), v(zr, NB), v(tr, NB),
                        v(n, n), v(NB, NB), b(n, 3 * NB), b(n, 3 * NB), b(n, n), b(n, n),
                        b(rows, n), b(rows, n), b(HOPS - 1, PIECES, part, n), b(HOPS, PIECES, part, n), b(2, part, n),
                        b(2, rows, n), b(rows, n), b(2, rows, n),
                        pltpu.SemaphoreType.DMA((COPIES,)), pltpu.SemaphoreType.DMA((COPIES,)),
                        pltpu.SemaphoreType.DMA((2, HOPS + 1, PIECES))],
        compiler_params=pltpu.CompilerParams(collective_id=0, has_side_effects=True, vmem_limit_bytes=60 * 2 ** 20),
        name="factor",
    )(grads, masks)


def shards(grads, round_masks):
    rows, width = grads.shape
    total = rows * lax.axis_size("row") * lax.axis_size("col")
    bit = [jnp.bitwise_and(jnp.right_shift(round_masks[0], b), 1) for b in range(HOPS)]
    flags = jnp.stack([bit[3] == bit[4], bit[1] != bit[2], bit[2] == bit[3], bit[0] == bit[2], bit[0] == 1,
                       bit[4] == bit[2], bit[0] == bit[3]]).astype(BF)
    masks = jnp.broadcast_to(jnp.repeat(flags, 16)[:, None], (flags.shape[0] * 16, width))
    return mega(grads, masks, total) * (1.0 / width ** 0.5)


def solution(mesh):
    return jax.shard_map(
        shards,
        mesh=mesh,
        in_specs=(P(("row", "col"), None), P()),
        out_specs=P(None, ("row", "col"), None),
        check_vma=False,
    )
```
